32 devices in a mesh: seq: 16 (over z, y, core), rep: 2 (over x).
Axes of the slice: x: 2, y: 2, z: 4, core: 2. Of those that a mesh axis runs over, the one named last changes fastest.
Arguments:
- queries: bfloat16 [2, 2, 1024, 1024], P('rep', None, 'seq'), may hold values from -5.5 to 5.5
- keys_values: bfloat16 [2, 2, 2, 1024, 512], P('rep', None, None, 'seq'), may hold values from -16 to 16
- block_lengths: int32 [2, 16], P('rep'), may hold values from 1 to 128, 1024 in all within a row
- out_weight: bfloat16 [1024, 1024], P('rep'), may hold values from -0.1875 to 0.1875
- cotangent: bfloat16 [2, 2, 1024, 1024], P('rep', None, 'seq'), may hold values from -0.5 to 0.5
Outputs:
- projected: bfloat16 [2, 2, 1024, 1024], P('rep', None, 'seq')
- weight_grad: float32 [1024, 1024], P('rep')
The draws below stay inside these ranges and needn't reach their ends.
Inputs may be any that keep to these rules, and one draw needn't show every extreme that they name: `block_lengths`: in each document the 16 block lengths sum to 1024 and the longest is exactly 128.
All inputs are finite; a program needn't handle non-finite values.
Results may differ from the reference program's by a relative error of at most 0.006.
Values may be sent and summed in bfloat16 or wider, within the bound.
A program may use at most 128 MiB of HBM per device.

```python
import math
import jax
import jax.numpy as jnp
import numpy as np
from jax import lax

HEADS = 8
KVH = 4
HD = 128
DOUT = 1024
LENGTH = 1024
DOCS = 2
NBLK = 16
BLOCK_MOST = 128
HW = 1024


def draw_queries(key, part):
    base = jax.random.normal(jax.random.fold_in(key, 11), (DOCS, 2, LENGTH, HEADS * HD), dtype=jnp.float32)
    return jnp.clip(base, -5.5, 5.5).astype(jnp.bfloat16)


def draw_keys_values(key, part):
    base = jax.random.normal(jax.random.fold_in(key, 23), (DOCS, 2, 2, LENGTH, KVH * HD), dtype=jnp.float32)
    factors = jnp.array([2.0, 3.0], dtype=jnp.float32).reshape(1, 1, 2, 1, 1)
    base = base * factors
    return jnp.clip(base, -16.0, 16.0).astype(jnp.bfloat16)


def with_spikes(entries, key, source, target, parts, factor):
    owner, partner = [(jnp.arange(entries.shape[dim]) // (entries.shape[dim] // parts)).reshape([-1 if axis == dim else 1 for axis in range(entries.ndim)]) for dim in (source, target)]
    chosen = jax.random.permutation(key, parts)[partner]
    strong = (owner == chosen) | (owner == (partner + parts // 2) % parts)
    return jnp.where(strong, factor * entries, entries)


def block_levels(stream_key, shape, split, least, top_value):
    def one(axis_at, blocks):
        draws = jax.random.uniform(jax.random.fold_in(jax.random.fold_in(stream_key, 6), axis_at), (blocks,), jnp.float32, least / len(split), top_value / len(split))
        return jnp.repeat(jnp.exp(draws), shape[axis_at] // blocks).reshape((-1,) + (1,) * (len(shape) - axis_at - 1))

    factor_of = one(*split[0])
    for cut in split[1:]:
        factor_of = factor_of * one(*cut)
    return factor_of


def split_up(amount, total, reach, slope):
    loads = [(1 << 20) // math.isqrt(grade ** slope) + 1 for grade in range(2, amount + 1)]
    spare, counts = total - reach - (amount - 1), [1] * (amount - 1)
    while spare > 0:
        candidates = [i for i in range(amount - 1) if counts[i] < reach]
        pool, remaining = sum([loads[i] for i in candidates]), spare
        for i in candidates:
            addition = min(reach - counts[i], max(1, remaining * loads[i] // pool), spare)
            counts[i] = counts[i] + addition
            spare = spare - addition
    return np.array([reach] + counts)


def uneven_parts(key, count, total, limit, skew):
    if count == 2:
        one = jax.random.randint(key, (), max(1, total - limit), min(limit, total - 1) + 1)
        return jnp.stack([one, total - one])
    tallies = jnp.asarray(split_up(count, total, limit, skew), jnp.int32)
    pairs = (count - 1) // 2
    giver, taker = tallies[1:1 + 2 * pairs:2], tallies[2:2 + 2 * pairs:2]
    margin = jnp.minimum(giver - 1, limit - taker)
    shifted = jax.random.randint(jax.random.fold_in(key, 1), (pairs,), 0, 1 << 20) % (margin + 1)
    tallies = tallies.at[1:1 + 2 * pairs:2].set(giver - shifted).at[2:2 + 2 * pairs:2].set(taker + shifted)
    return tallies[jax.random.permutation(jax.random.fold_in(key, 2), count)]


def gaussian(key, shape, width, limit, cuts=(), kind=jnp.bfloat16):
    drawn = jax.random.normal(key, shape, jnp.float32) * width
    if len(cuts) > 0:
        drawn = block_levels(key, shape, cuts, -0.22, 0.18) * drawn
    return jnp.clip(drawn, min=-limit, max=limit).astype(kind)


def heavy_noise(own_key, extent, scale, limit, shards, heavy, kind=jnp.bfloat16):
    entries = scale * jax.random.normal(own_key, extent, jnp.float32)
    if shards:
        entries = entries * block_levels(own_key, extent, shards, -0.22, 0.18)
    return jnp.clip(with_spikes(entries, jax.random.fold_in(own_key, 3), *heavy), -limit, limit).astype(kind)


def setup_inputs(seed: int = 0) -> dict:
    keys = jax.random.split(jax.random.key(seed), 6)
    return {
        "queries": draw_queries(jax.random.fold_in(keys[5], 71), 0),
        "keys_values": draw_keys_values(jax.random.fold_in(keys[5], 71), 0),
        "block_lengths": jax.vmap(lambda own: uneven_parts(own, NBLK, LENGTH, BLOCK_MOST, 2))(jax.random.split(keys[2], DOCS)).reshape((DOCS, NBLK)).astype(jnp.int32),
        "out_weight": gaussian(keys[3], (HW, DOUT), HW ** -0.5, 0.1875, ((0, 2),)),
        "cotangent": heavy_noise(keys[4], (DOCS, 2, LENGTH, DOUT), (4.0 * (2 * LENGTH * DOCS) ** -0.5), 0.5, ((0, 2), (2, 16)), (2, 3, 16, 2.0)),
    }


NEG_BIG = -1e+30

def block_index(block_ends, positions):
    return lax.optimization_barrier(jnp.sum((block_ends[None, :] <= positions[:, None]).astype(jnp.int32), axis=1)).astype(jnp.int32)

def one_document(inputs):
    doc_queries, doc_kv, doc_lengths = inputs
    group_size = HEADS // KVH
    score_scale = 1.0 / math.sqrt(HD)
    block_ends = jnp.cumsum(doc_lengths).astype(jnp.int32)
    positions = jnp.arange(LENGTH, dtype=jnp.int32)
    blocks = block_index(block_ends, positions)
    all_blocks = jnp.concatenate([blocks, blocks])
    all_copies = jnp.concatenate([jnp.zeros((LENGTH,), jnp.int32), jnp.ones((LENGTH,), jnp.int32)])
    key_rows = doc_kv[:, 0].reshape(2 * LENGTH, KVH, HD).astype(jnp.float32)
    value_rows = doc_kv[:, 1].reshape(2 * LENGTH, KVH, HD).astype(jnp.float32)
    query_rows = doc_queries.reshape(2 * LENGTH, KVH, group_size, HD)
    slab = math.gcd(512, 2 * LENGTH)

    def one_slab(index):
        row_start = (index * slab).astype(jnp.int32)
        slab_queries = lax.dynamic_slice_in_dim(query_rows, row_start, slab, 0).astype(jnp.float32)
        slab_blocks = lax.dynamic_slice_in_dim(all_blocks, row_start, slab, 0)
        slab_copies = lax.dynamic_slice_in_dim(all_copies, row_start, slab, 0)
        scores = jnp.einsum('qgjd,kgd->gjqk', slab_queries, key_rows) * score_scale
        noisy_allowed = (all_copies[None, :] == 0) & (all_blocks[None, :] == slab_blocks[:, None]) | (all_copies[None, :] == 1) & (all_blocks[None, :] < slab_blocks[:, None])
        clean_allowed = (all_copies[None, :] == 1) & (all_blocks[None, :] <= slab_blocks[:, None])
        allowed = jnp.where(slab_copies[:, None] == 0, noisy_allowed, clean_allowed)
        masked = jnp.where(allowed, scores, NEG_BIG)
        row_max = lax.optimization_barrier(jnp.max(masked, axis=-1, keepdims=True))
        weights = jnp.where(allowed, jnp.exp(masked - row_max), 0.0)
        totals = lax.optimization_barrier(jnp.sum(weights, axis=-1))
        rounded = lax.optimization_barrier(weights.astype(jnp.bfloat16)).astype(jnp.float32)
        summed = jnp.einsum('gjqk,kgd->gjqd', rounded, value_rows)
        attended = (summed / totals[..., None]).transpose(2, 0, 1, 3).reshape(slab, HEADS * HD)
        return attended.astype(jnp.bfloat16)
    slabs = lax.map(one_slab, jnp.arange(2 * LENGTH // slab, dtype=jnp.int32))
    return slabs.reshape(2, LENGTH, HEADS * HD)

def reference(queries, keys_values, block_lengths, out_weight, cotangent):
    attended = lax.map(one_document, (queries, keys_values, block_lengths))
    flat = attended.reshape(DOCS * 2 * LENGTH, HEADS * HD)
    projected = jnp.dot(flat, out_weight, preferred_element_type=jnp.float32).astype(jnp.bfloat16)
    projected = projected.reshape(DOCS, 2, LENGTH, DOUT)
    weight_grad = jnp.dot(flat.T, cotangent.reshape(DOCS * 2 * LENGTH, DOUT), preferred_element_type=jnp.float32)
    return (projected, weight_grad)
```

```python
import functools
import math

import jax
import jax.numpy as jnp
from jax import lax
from jax.experimental import pallas as pl
from jax.experimental.pallas import tpu as pltpu
from jax.sharding import PartitionSpec as P

HD = 128
NEG = -1e30
MESH = pl.DeviceIdType.MESH
F32 = jnp.float32
BF16 = jnp.bfloat16


def kernel(
    ns, nr, nc,
    len_ref, q_ref, kv_ref, w_ref, cot_ref,
    proj_ref, wg_ref,
    kvc, kvn, wbuf, cbuf, abuf, att_t, att, acc, m_ref, l_ref, gbuf, rbuf, fbuf,
    loc, kv_rx, kv_zs, kv_ys, kv_cs, n_rx, n_tx, w_rx, w_tx, w_cs,
    c_rx, c_rs, c_ys, c_cs, a_rx, a_tx, g_rx, g_tx, f_rx, f_zs, f_ys, f_cs,
):
    nz = ns // 4
    grp = 4 * nr
    rows = q_ref.shape[1]
    qn = 2 * rows
    heads = q_ref.shape[2] // HD
    kvh = kv_ref.shape[4] // HD
    gs = heads // kvh
    lanes = gs * qn
    nblk = len_ref.shape[1]
    slice_rows = abuf.shape[1]
    cr, cc = gbuf.shape[1], gbuf.shape[2]
    w_half = wbuf.shape[2]

    s = lax.axis_index("seq")
    r = lax.axis_index("rep")
    k = lax.rem(s, 2)
    y = lax.rem(s // 2, 2)
    z = s // 4
    base = 4 * z
    y_peer = base + 2 * (1 - y) + k
    c_peer = base + 2 * y + 1 - k

    def seq_id(zz, yy, kk):
        return 4 * zz + 2 * yy + kk

    def rcopy(src, dst, tx, rx, seq, rep=None):
        return pltpu.make_async_remote_copy(
            src_ref=src, dst_ref=dst, send_sem=tx, recv_sem=rx,
            device_id=(seq, r if rep is None else rep), device_id_type=MESH,
        )

    barrier = pltpu.get_barrier_semaphore()

    @pl.loop(0, ns)
    def _(i):
        @pl.when(i != s)
        def _():
            pl.semaphore_signal(barrier, inc=1, device_id=(i, r), device_id_type=MESH)

    for j in range(nr):
        @pl.when(j != r)
        def _():
            for q in range(4):
                pl.semaphore_signal(
                    barrier, inc=1, device_id=(base + q, j), device_id_type=MESH
                )

    own_kv = pltpu.make_async_copy(kv_ref.at[0, 1], kvc.at[s], loc.at[0])
    own_n = pltpu.make_async_copy(kv_ref.at[0, 0], kvn.at[2], loc.at[1])
    own_w = [
        pltpu.make_async_copy(
            w_ref.at[pl.ds(h * w_half, w_half)], wbuf.at[r, h], loc.at[2 + h]
        )
        for h in range(2)
    ]
    me = r * 4 + 2 * y + k
    own_c = pltpu.make_async_copy(cot_ref.at[0], cbuf.at[me], loc.at[4])
    for cp in [own_kv, own_n, own_c] + own_w:
        cp.start()

    pl.semaphore_wait(barrier, ns - 1 + 4 * (nr - 1))

    clean = kv_ref.at[0, 1]

    def kv_z(zz):
        return rcopy(clean, kvc.at[s], kv_zs.at[zz], kv_rx.at[s], seq_id(zz, y, k))

    def kv_y(zz):
        slot = seq_id(zz, y, k)
        return rcopy(kvc.at[slot], kvc.at[slot], kv_ys.at[zz], kv_rx.at[slot], y_peer)

    def kv_c(zz, yy):
        slot = seq_id(zz, yy, k)
        return rcopy(
            kvc.at[slot], kvc.at[slot], kv_cs.at[2 * zz + yy], kv_rx.at[slot], c_peer
        )

    def kv_wait(zz, yy, kk):
        slot = seq_id(zz, yy, kk)
        rcopy(kvc.at[slot], kvc.at[slot], kv_zs.at[0], kv_rx.at[slot], c_peer).wait_recv()

    kv_own_y = rcopy(clean, kvc.at[s], kv_ys.at[z], kv_rx.at[s], y_peer)
    kv_own_c = rcopy(clean, kvc.at[s], kv_cs.at[2 * z + y], kv_rx.at[s], c_peer)

    @pl.loop(z + 1, nz)
    def _(zz):
        kv_z(zz).start()

    kv_own_y.start()
    kv_own_c.start()

    @pl.when(z > 0)
    def _():
        kv_z(z - 1).start()

    noisy_steps = ((1, 0), (-1, 1), (2, 2), (-2, 3))

    def inside(step):
        return (s + step >= 0) & (s + step < ns)

    def noisy_tx(step, i):
        return rcopy(
            kv_ref.at[0, 0], kvn.at[2 - step], n_tx.at[i], n_rx.at[2 - step], s + step
        )

    for step, i in noisy_steps:
        @pl.when(inside(step))
        def _():
            noisy_tx(step, i).start()

        @pl.when(jnp.logical_not(inside(step)))
        def _():
            kvn[2 + step] = jnp.zeros(kvn.shape[1:], kvn.dtype)

    def c_rep(j):
        return rcopy(cot_ref.at[0], cbuf.at[me], c_rs.at[j], c_rx.at[me], s, j)

    def w_rep(j):
        return rcopy(
            w_ref.at[pl.ds(pl.multiple_of(k * w_half, w_half), w_half)],
            wbuf.at[r, k], w_tx.at[j], w_rx.at[r, k], s, j,
        )

    for j in range(nr):
        @pl.when(j != r)
        def _():
            c_rep(j).start()
            w_rep(j).start()

    lane = lax.broadcasted_iota(jnp.int32, (1, lanes), 1)
    qi = lax.rem(lane, qn)
    noisy = qi < rows
    qpos = s * rows + lax.rem(qi, rows)

    def find(b, carry):
        prev, start, end = carry
        stop = prev + len_ref[0, b]
        hit = (qpos >= prev) & (qpos < stop)
        return stop, jnp.where(hit, prev, start), jnp.where(hit, stop, end)

    zero_row = jnp.zeros((1, lanes), jnp.int32)
    _, start, end = lax.fori_loop(0, nblk, find, (jnp.int32(0), zero_row, zero_row))
    clean_hi = jnp.where(noisy, start, end)
    noisy_lo = jnp.where(noisy, start, 0)
    noisy_hi = jnp.where(noisy, end, 0)

    m_ref[...] = jnp.full(m_ref.shape, NEG, F32)
    l_ref[...] = jnp.zeros(l_ref.shape, F32)
    acc[...] = jnp.zeros(acc.shape, F32)
    score_scale = math.log2(math.e) / math.sqrt(HD)

    def absorb(load, allowed):
        for g in range(kvh):
            keys = load(0, g)
            vals = load(1, g)
            qg = jnp.concatenate(
                [
                    q_ref[:, :, (g * gs + j) * HD:(g * gs + j + 1) * HD].reshape(qn, HD)
                    for j in range(gs)
                ],
                axis=0,
            )
            sc = lax.dot_general(
                keys, qg, (((1,), (1,)), ((), ())), preferred_element_type=F32
            )
            sc = jnp.where(allowed, sc * score_scale, NEG)
            m_old = m_ref[g]
            m_new = jnp.maximum(m_old, jnp.max(sc, axis=0, keepdims=True))
            m_use = jnp.maximum(m_new, NEG / 2)
            p = jnp.exp2(sc - m_use)
            f = jnp.exp2(m_old - m_use)
            m_ref[g] = m_new
            l_ref[g] = l_ref[g] * f + jnp.sum(p, axis=0, keepdims=True)
            up = lax.dot_general(
                vals, p.astype(BF16), (((0,), (0,)), ((), ())), preferred_element_type=F32
            )
            acc[g] = acc[g] * f + up

    own_kv.wait()
    own_n.wait()
    for step, i in noisy_steps:
        @pl.when(inside(step))
        def _():
            rcopy(
                kvn.at[2 + step], kvn.at[2 + step], n_tx.at[i], n_rx.at[2 + step], c_peer
            ).wait_recv()

    kp_n = (s - 2) * rows + lax.broadcasted_iota(jnp.int32, (5 * rows, lanes), 0)
    absorb(
        lambda a, g: kvn[:, a, :, g * HD:(g + 1) * HD].reshape(5 * rows, HD),
        (kp_n >= noisy_lo) & (kp_n < noisy_hi),
    )

    order = list(range(nz - 1, -1, -1))
    for i in range(nz + 2):
        if i < nz:
            zz = order[i]

            @pl.when((zz <= z + 1) & (zz != z))
            def _():
                kv_wait(zz, y, k)
                kv_y(zz).start()
                kv_c(zz, y).start()

        if 1 <= i <= nz:
            zz = order[i - 1]

            @pl.when(zz <= z + 1)
            def _():
                kv_wait(zz, 1 - y, k)
                kv_c(zz, 1 - y).start()

        if i >= 2:
            zz = order[i - 2]

            @pl.when(zz <= z + 1)
            def _():
                kv_wait(zz, y, 1 - k)
                kv_wait(zz, 1 - y, 1 - k)
                kp = zz * (4 * rows) + lax.broadcasted_iota(
                    jnp.int32, (4 * rows, lanes), 0
                )
                absorb(
                    lambda a, g: kvc[4 * zz:4 * zz + 4, a, :, g * HD:(g + 1) * HD].reshape(
                        4 * rows, HD
                    ),
                    kp < clean_hi,
                )

    def c_slot(j, yy, kk):
        return j * 4 + 2 * yy + kk

    def c_fwd(slot, tx, peer):
        return rcopy(cbuf.at[slot], cbuf.at[slot], tx, c_rx.at[slot], peer)

    own_c.wait()
    for j in range(nr):
        @pl.when(j != r)
        def _():
            c_fwd(c_slot(j, y, k), c_rs.at[j], c_peer).wait_recv()
        c_fwd(c_slot(j, y, k), c_ys.at[j], y_peer).start()
        c_fwd(c_slot(j, y, k), c_cs.at[2 * j], c_peer).start()

    for g in range(kvh):
        o = acc[g] / l_ref[g]
        for j in range(gs):
            h = g * gs + j
            part = o[:, j * qn:(j + 1) * qn]
            att_t[h * HD:(h + 1) * HD, :] = part.astype(BF16)
            att[:, h * HD:(h + 1) * HD] = part.T.astype(BF16)

    def a_copy(j, q):
        i = j * 4 + q
        return rcopy(
            att_t.at[pl.ds(i * slice_rows, slice_rows)], abuf.at[me], a_tx.at[i],
            a_rx.at[me], base + q, j,
        )

    for j in range(nr):
        for q in range(4):
            i = j * 4 + q

            @pl.when(i != me)
            def _():
                a_copy(j, q).start()

    abuf[me] = att_t[pl.ds(pl.multiple_of(me * slice_rows, slice_rows), slice_rows), :]

    for cp in own_w:
        cp.wait()

    def w_fwd(j, h, tx):
        return rcopy(wbuf.at[j, h], wbuf.at[j, h], tx, w_rx.at[j, h], c_peer)

    for j in range(nr):
        @pl.when(j != r)
        def _():
            w_fwd(j, k, w_tx.at[j]).wait_recv()
            w_fwd(j, k, w_cs.at[j]).start()
    for j in range(nr):
        c_fwd(c_slot(j, 1 - y, k), c_rs.at[0], c_peer).wait_recv()
        c_fwd(c_slot(j, 1 - y, k), c_cs.at[2 * j + 1], c_peer).start()
    for j in range(nr):
        @pl.when(j != r)
        def _():
            w_fwd(j, 1 - k, w_tx.at[j]).wait_recv()

    tile = 256
    for t in range(wbuf.shape[3] // tile):
        cols = slice(t * tile, (t + 1) * tile)
        w_tile = wbuf[:, :, :, cols].reshape(heads * HD, tile)
        proj_ref[:, :, cols] = (
            jnp.dot(att[...], w_tile, preferred_element_type=F32)
            .astype(BF16).reshape(2, rows, tile)
        )

    for j in range(nr):
        for yy in range(2):
            c_fwd(c_slot(j, yy, 1 - k), c_rs.at[0], c_peer).wait_recv()
    for j in range(nr):
        for q in range(4):
            i = j * 4 + q

            @pl.when(i != me)
            def _():
                rcopy(abuf.at[i], abuf.at[i], a_tx.at[i], a_rx.at[i], c_peer).wait_recv()

    def g_copy(zz):
        return rcopy(
            gbuf.at[zz], rbuf.at[z], g_tx.at[zz], g_rx.at[z], seq_id(zz, y, k)
        )

    lhs = jnp.concatenate([abuf[i] for i in range(grp)], axis=1)
    for cb in range(nc):
        rhs = cbuf[:, :, :, cb * cc:(cb + 1) * cc].reshape(grp * qn, cc)
        g_tile = jnp.dot(lhs, rhs, preferred_element_type=F32).astype(BF16)
        for rr in range(nz // nc):
            zz = rr * nc + cb
            gbuf[zz] = g_tile[rr * cr:(rr + 1) * cr]

            @pl.when(zz != z)
            def _():
                g_copy(zz).start()

            @pl.when(zz == z)
            def _():
                rbuf[zz] = g_tile[rr * cr:(rr + 1) * cr]

    total = jnp.zeros((cr, cc), F32)
    for zz in range(nz):
        @pl.when(zz != z)
        def _():
            rcopy(rbuf.at[zz], rbuf.at[zz], g_tx.at[zz], g_rx.at[zz], c_peer).wait_recv()

        total = total + rbuf[zz].astype(F32)

    def region(zz, yy, kk):
        return fbuf.at[seq_id(zz, yy, kk)]

    fbuf[s] = total.astype(BF16)

    def f_copy(zz, yy, kk, tx, peer):
        return rcopy(
            region(zz, yy, kk), region(zz, yy, kk), tx, f_rx.at[seq_id(zz, yy, kk)], peer
        )

    def f_z(zz):
        return f_copy(z, y, k, f_zs.at[zz], seq_id(zz, y, k))

    for zz in range(nz):
        @pl.when(zz != z)
        def _():
            f_z(zz).start()
    f_copy(z, y, k, f_ys.at[z], y_peer).start()
    f_copy(z, y, k, f_cs.at[2 * z + y], c_peer).start()
    for zz in range(nz):
        @pl.when(zz != z)
        def _():
            f_copy(zz, y, k, f_ys.at[zz], y_peer).wait_recv()
            f_copy(zz, y, k, f_ys.at[zz], y_peer).start()
            f_copy(zz, y, k, f_cs.at[2 * zz + y], c_peer).start()
    for zz in range(nz):
        f_copy(zz, 1 - y, k, f_cs.at[0], c_peer).wait_recv()
        f_copy(zz, 1 - y, k, f_cs.at[2 * zz + 1 - y], c_peer).start()
    for zz in range(nz):
        for yy in range(2):
            f_copy(zz, yy, 1 - k, f_cs.at[0], c_peer).wait_recv()

    for slot in range(ns):
        zz, q = slot // 4, slot % 4
        row = q * slice_rows + (zz // nc) * cr
        col = (zz % nc) * cc
        wg_ref[row:row + cr, col:col + cc] = fbuf[slot]

    @pl.loop(z + 1, nz)
    def _(zz):
        kv_z(zz).wait_send()

    @pl.when(z > 0)
    def _():
        kv_z(z - 1).wait_send()

    for zz in range(nz):
        @pl.when(zz <= z + 1)
        def _():
            kv_y(zz).wait_send()
            kv_c(zz, 0).wait_send()
            kv_c(zz, 1).wait_send()

    for step, i in noisy_steps:
        @pl.when(inside(step))
        def _():
            noisy_tx(step, i).wait_send()
    for j in range(nr):
        @pl.when(j != r)
        def _():
            c_rep(j).wait_send()
            w_rep(j).wait_send()
            w_fwd(j, k, w_cs.at[j]).wait_send()
        c_fwd(c_slot(j, y, k), c_ys.at[j], y_peer).wait_send()
        for h in range(2):
            c_fwd(c_slot(j, h, k), c_cs.at[2 * j + h], c_peer).wait_send()
        for q in range(4):
            @pl.when(j * 4 + q != me)
            def _():
                a_copy(j, q).wait_send()
    for zz in range(nz):
        @pl.when(zz != z)
        def _():
            g_copy(zz).wait_send()
            f_z(zz).wait_send()
        f_copy(zz, y, k, f_ys.at[zz], y_peer).wait_send()
        for yy in range(2):
            f_copy(zz, yy, k, f_cs.at[2 * zz + yy], c_peer).wait_send()


def on_device(queries, keys_values, block_lengths, out_weight, cotangent):
    ns, nr = lax.axis_size("seq"), lax.axis_size("rep")
    nz = ns // 4
    rows, q_width = queries.shape[2], queries.shape[3]
    kv_width = keys_values.shape[4]
    w_rows, out_width = out_weight.shape
    kvh, gs = kv_width // HD, q_width // kv_width
    qn = 2 * rows
    lanes = gs * qn
    slice_rows = w_rows // 4
    nc = min(nz, out_width // 128)
    cr, cc = slice_rows // (nz // nc), out_width // nc
    dma = pltpu.SemaphoreType.DMA
    vmem, hbm = pl.BlockSpec(memory_space=pltpu.VMEM), pl.BlockSpec(memory_space=pl.ANY)
    projected, grad = pl.pallas_call(
        functools.partial(kernel, ns, nr, nc),
        out_shape=(
            jax.ShapeDtypeStruct((2, rows, out_width), BF16),
            jax.ShapeDtypeStruct((w_rows, out_width), BF16),
        ),
        in_specs=[pl.BlockSpec(memory_space=pltpu.SMEM), vmem, hbm, hbm, hbm],
        out_specs=(vmem, vmem),
        scratch_shapes=[
            pltpu.VMEM((ns, 2, rows, kv_width), BF16),
            pltpu.VMEM((5, 2, rows, kv_width), BF16),
            pltpu.VMEM((nr, 2, w_rows // 2, out_width), BF16),
            pltpu.VMEM((4 * nr, 2, rows, out_width), BF16),
            pltpu.VMEM((4 * nr, slice_rows, qn), BF16),
            pltpu.VMEM((q_width, qn), BF16),
            pltpu.VMEM((qn, q_width), BF16),
            pltpu.VMEM((kvh, HD, lanes), F32),
            pltpu.VMEM((kvh, 1, lanes), F32),
            pltpu.VMEM((kvh, 1, lanes), F32),
            pltpu.VMEM((nz, cr, cc), BF16),
            pltpu.VMEM((nz, cr, cc), BF16),
            pltpu.VMEM((ns, cr, cc), BF16),
            dma((5,)),
            dma((ns,)), dma((nz,)), dma((nz,)), dma((ns // 2,)),
            dma((5,)), dma((4,)),
            dma((nr, 2)), dma((nr,)), dma((nr,)),
            dma((4 * nr,)), dma((nr,)), dma((nr,)), dma((2 * nr,)),
            dma((4 * nr,)), dma((4 * nr,)),
            dma((nz,)), dma((nz,)),
            dma((ns,)), dma((nz,)), dma((nz,)), dma((ns // 2,)),
        ],
        compiler_params=pltpu.CompilerParams(
            collective_id=0, has_side_effects=True, vmem_limit_bytes=60 * 2**20
        ),
    )(block_lengths, queries[0], keys_values, out_weight, cotangent)
    return projected[None], grad.astype(F32)


def solution(mesh):
    placed = (
        P("rep", None, "seq", None),
        P("rep", None, None, "seq", None),
        P("rep", None),
        P("rep", None),
        P("rep", None, "seq", None),
    )
    return jax.shard_map(
        on_device,
        mesh=mesh,
        in_specs=placed,
        out_specs=(P("rep", None, "seq", None), P("rep", None)),
        check_vma=False,
    )
```

```python
import functools
import math

import jax
import jax.numpy as jnp
from jax import lax
from jax.experimental import pallas as pl
from jax.experimental.pallas import tpu as pltpu
from jax.sharding import PartitionSpec as P

HD = 128
NEG = -1e30
MESH = pl.DeviceIdType.MESH
F32 = jnp.float32
BF16 = jnp.bfloat16


def kernel(
    ns, nr, nc,
    len_ref, q_ref, kv_ref, w_ref, cot_ref,
    proj_ref, wg_ref,
    kvc, kvn, wbuf, cbuf, abuf, att_t, att, acc, m_ref, l_ref, gbuf, rbuf, fbuf,
    loc, kv_rx, kv_zs, kv_ys, kv_cs, n_rx, n_tx, w_rx, w_tx, w_cs,
    c_rx, c_rs, c_ys, c_cs, a_rx, a_tx, g_rx, g_tx, f_rx, f_zs, f_ys, f_cs,
):
    nz = ns // 4
    grp = 4 * nr
    rows = q_ref.shape[1]
    qn = 2 * rows
    heads = q_ref.shape[2] // HD
    kvh = kv_ref.shape[4] // HD
    gs = heads // kvh
    lanes = gs * qn
    nblk = len_ref.shape[1]
    slice_rows = abuf.shape[1]
    cr, cc = gbuf.shape[1], gbuf.shape[2]
    w_half = wbuf.shape[2]

    s = lax.axis_index("seq")
    r = lax.axis_index("rep")
    k = lax.rem(s, 2)
    y = lax.rem(s // 2, 2)
    z = s // 4
    base = 4 * z
    y_peer = base + 2 * (1 - y) + k
    c_peer = base + 2 * y + 1 - k

    def seq_id(zz, yy, kk):
        return 4 * zz + 2 * yy + kk

    def rcopy(src, dst, tx, rx, seq, rep=None):
        return pltpu.make_async_remote_copy(
            src_ref=src, dst_ref=dst, send_sem=tx, recv_sem=rx,
            device_id=(seq, r if rep is None else rep), device_id_type=MESH,
        )

    barrier = pltpu.get_barrier_semaphore()

    @pl.loop(0, ns)
    def _(i):
        @pl.when(i != s)
        def _():
            pl.semaphore_signal(barrier, inc=1, device_id=(i, r), device_id_type=MESH)

    for j in range(nr):
        @pl.when(j != r)
        def _():
            for q in range(4):
                pl.semaphore_signal(
                    barrier, inc=1, device_id=(base + q, j), device_id_type=MESH
                )

    own_kv = pltpu.make_async_copy(kv_ref.at[0, 1], kvc.at[s], loc.at[0])
    own_n = pltpu.make_async_copy(kv_ref.at[0, 0], kvn.at[2], loc.at[1])
    own_w = [
        pltpu.make_async_copy(
            w_ref.at[pl.ds(h * w_half, w_half)], wbuf.at[r, h], loc.at[2 + h]
        )
        for h in range(2)
    ]
    me = r * 4 + 2 * y + k
    own_c = pltpu.make_async_copy(cot_ref.at[0], cbuf.at[me], loc.at[4])
    for cp in [own_kv, own_n, own_c] + own_w:
        cp.start()

    pl.semaphore_wait(barrier, ns - 1 + 4 * (nr - 1))

    clean = kv_ref.at[0, 1]

    def kv_z(zz):
        return rcopy(clean, kvc.at[s], kv_zs.at[zz], kv_rx.at[s], seq_id(zz, y, k))

    def kv_y(zz):
        slot = seq_id(zz, y, k)
        return rcopy(kvc.at[slot], kvc.at[slot], kv_ys.at[zz], kv_rx.at[slot], y_peer)

    def kv_c(zz, yy):
        slot = seq_id(zz, yy, k)
        return rcopy(
            kvc.at[slot], kvc.at[slot], kv_cs.at[2 * zz + yy], kv_rx.at[slot], c_peer
        )

    def kv_wait(zz, yy, kk):
        slot = seq_id(zz, yy, kk)
        rcopy(kvc.at[slot], kvc.at[slot], kv_zs.at[0], kv_rx.at[slot], c_peer).wait_recv()

    kv_own_y = rcopy(clean, kvc.at[s], kv_ys.at[z], kv_rx.at[s], y_peer)
    kv_own_c = rcopy(clean, kvc.at[s], kv_cs.at[2 * z + y], kv_rx.at[s], c_peer)

    @pl.loop(z + 1, nz)
    def _(zz):
        kv_z(zz).start()

    kv_own_y.start()
    kv_own_c.start()

    @pl.when(z > 0)
    def _():
        kv_z(z - 1).start()

    noisy_steps = ((2, 0), (-2, 1))
    own_noisy = kv_ref.at[0, 0]

    def inside(step):
        return (s + step >= 0) & (s + step < ns)

    def noisy_tx(step, i):
        return rcopy(own_noisy, kvn.at[2 - step], n_tx.at[i], n_rx.at[2 - step], s + step)

    def noisy_c(src, slot, i):
        return rcopy(src, kvn.at[slot], n_tx.at[i], n_rx.at[slot], c_peer)

    def noisy_wait(slot):
        rcopy(kvn.at[slot], kvn.at[slot], n_tx.at[0], n_rx.at[slot], c_peer).wait_recv()

    for step, i in noisy_steps:
        @pl.when(inside(step))
        def _():
            noisy_tx(step, i).start()

        @pl.when(jnp.logical_not(inside(step)))
        def _():
            kvn[2 + step] = jnp.zeros(kvn.shape[1:], kvn.dtype)

    @pl.when(k == 0)
    def _():
        noisy_c(own_noisy, 1, 2).start()

    @pl.when(k == 1)
    def _():
        noisy_c(own_noisy, 3, 2).start()

    @pl.when((k == 0) & (s == 0))
    def _():
        kvn[1] = jnp.zeros(kvn.shape[1:], kvn.dtype)

    @pl.when((k == 1) & (s == ns - 1))
    def _():
        kvn[3] = jnp.zeros(kvn.shape[1:], kvn.dtype)

    def noisy_relay(finish):
        for kk, step, slot in ((0, 2, 3), (1, -2, 1)):
            @pl.when((k == kk) & inside(step))
            def _():
                copy = noisy_c(kvn.at[2 + step], slot, 3)
                if finish:
                    copy.wait_send()
                else:
                    noisy_wait(2 + step)
                    copy.start()

    def c_rep(j):
        return rcopy(cot_ref.at[0], cbuf.at[me], c_rs.at[j], c_rx.at[me], s, j)

    def w_rep(j):
        return rcopy(
            w_ref.at[pl.ds(pl.multiple_of(k * w_half, w_half), w_half)],
            wbuf.at[r, k], w_tx.at[j], w_rx.at[r, k], s, j,
        )

    for j in range(nr):
        @pl.when(j != r)
        def _():
            c_rep(j).start()
            w_rep(j).start()

    lane = lax.broadcasted_iota(jnp.int32, (1, lanes), 1)
    qi = lax.rem(lane, qn)
    noisy = qi < rows
    qpos = s * rows + lax.rem(qi, rows)

    def find(b, carry):
        prev, start, end = carry
        stop = prev + len_ref[0, b]
        hit = (qpos >= prev) & (qpos < stop)
        return stop, jnp.where(hit, prev, start), jnp.where(hit, stop, end)

    zero_row = jnp.zeros((1, lanes), jnp.int32)
    _, start, end = lax.fori_loop(0, nblk, find, (jnp.int32(0), zero_row, zero_row))
    clean_hi = jnp.where(noisy, start, end)
    noisy_lo = jnp.where(noisy, start, 0)
    noisy_hi = jnp.where(noisy, end, 0)

    m_ref[...] = jnp.full(m_ref.shape, NEG, F32)
    l_ref[...] = jnp.zeros(l_ref.shape, F32)
    acc[...] = jnp.zeros(acc.shape, F32)
    score_scale = math.log2(math.e) / math.sqrt(HD)

    def absorb(load, allowed):
        for g in range(kvh):
            keys = load(0, g)
            vals = load(1, g)
            qg = jnp.concatenate(
                [
                    q_ref[:, :, (g * gs + j) * HD:(g * gs + j + 1) * HD].reshape(qn, HD)
                    for j in range(gs)
                ],
                axis=0,
            )
            sc = lax.dot_general(
                keys, qg, (((1,), (1,)), ((), ())), preferred_element_type=F32
            )
            sc = jnp.where(allowed, sc * score_scale, NEG)
            m_old = m_ref[g]
            m_new = jnp.maximum(m_old, jnp.max(sc, axis=0, keepdims=True))
            m_use = jnp.maximum(m_new, NEG / 2)
            p = jnp.exp2(sc - m_use)
            f = jnp.exp2(m_old - m_use)
            m_ref[g] = m_new
            l_ref[g] = l_ref[g] * f + jnp.sum(p, axis=0, keepdims=True)
            up = lax.dot_general(
                vals, p.astype(BF16), (((0,), (0,)), ((), ())), preferred_element_type=F32
            )
            acc[g] = acc[g] * f + up

    kp_n = (s - 2) * rows + lax.broadcasted_iota(jnp.int32, (5 * rows, lanes), 0)

    def noisy_absorb():
        own_n.wait()

        for kk, step in ((0, -2), (1, 2)):
            @pl.when((k == kk) & inside(step))
            def _():
                noisy_wait(2 + step)

        for slot, kk, edge in ((1, 0, 0), (3, 1, ns - 1)):
            @pl.when((k == 1 - kk) | (s != edge))
            def _():
                noisy_wait(slot)

        absorb(
            lambda a, g: kvn[:, a, :, g * HD:(g + 1) * HD].reshape(5 * rows, HD),
            (kp_n >= noisy_lo) & (kp_n < noisy_hi),
        )

    def c_slot(j, yy, kk):
        return j * 4 + 2 * yy + kk

    def c_fwd(slot, tx, peer):
        return rcopy(cbuf.at[slot], cbuf.at[slot], tx, c_rx.at[slot], peer)

    own_kv.wait()
    order = list(range(nz - 1, -1, -1))
    for i in range(nz + 2):
        if i < nz:
            zz = order[i]

            @pl.when((zz <= z + 1) & (zz != z))
            def _():
                kv_wait(zz, y, k)
                kv_y(zz).start()
                kv_c(zz, y).start()

        if i == nz - 1:
            own_c.wait()
            for j in range(nr):
                @pl.when(j != r)
                def _():
                    c_fwd(c_slot(j, y, k), c_rs.at[j], c_peer).wait_recv()
                c_fwd(c_slot(j, y, k), c_ys.at[j], y_peer).start()

        if 1 <= i <= nz:
            zz = order[i - 1]

            @pl.when(zz <= z + 1)
            def _():
                kv_wait(zz, 1 - y, k)
                kv_c(zz, 1 - y).start()

        if i == nz - 1:
            noisy_relay(False)

        if i == nz:
            for j in range(nr):
                c_fwd(c_slot(j, y, k), c_cs.at[2 * j], c_peer).start()
            noisy_absorb()

        if i >= 2:
            zz = order[i - 2]

            @pl.when(zz <= z + 1)
            def _():
                kv_wait(zz, y, 1 - k)
                kv_wait(zz, 1 - y, 1 - k)
                kp = zz * (4 * rows) + lax.broadcasted_iota(
                    jnp.int32, (4 * rows, lanes), 0
                )
                absorb(
                    lambda a, g: kvc[4 * zz:4 * zz + 4, a, :, g * HD:(g + 1) * HD].reshape(
                        4 * rows, HD
                    ),
                    kp < clean_hi,
                )

    for g in range(kvh):
        o = acc[g] / l_ref[g]
        for j in range(gs):
            h = g * gs + j
            part = o[:, j * qn:(j + 1) * qn]
            att_t[h * HD:(h + 1) * HD, :] = part.astype(BF16)
            att[:, h * HD:(h + 1) * HD] = part.T.astype(BF16)

    def a_copy(j, q):
        i = j * 4 + q
        return rcopy(
            att_t.at[pl.ds(i * slice_rows, slice_rows)], abuf.at[me], a_tx.at[i],
            a_rx.at[me], base + q, j,
        )

    for j in range(nr):
        for q in range(4):
            i = j * 4 + q

            @pl.when(i != me)
            def _():
                a_copy(j, q).start()

    abuf[me] = att_t[pl.ds(pl.multiple_of(me * slice_rows, slice_rows), slice_rows), :]

    for cp in own_w:
        cp.wait()

    def w_fwd(j, h, tx):
        return rcopy(wbuf.at[j, h], wbuf.at[j, h], tx, w_rx.at[j, h], c_peer)

    for j in range(nr):
        @pl.when(j != r)
        def _():
            w_fwd(j, k, w_tx.at[j]).wait_recv()
            w_fwd(j, k, w_cs.at[j]).start()
    for j in range(nr):
        @pl.when(j != r)
        def _():
            w_fwd(j, 1 - k, w_tx.at[j]).wait_recv()

    tile = 256
    for t in range(wbuf.shape[3] // tile):
        cols = slice(t * tile, (t + 1) * tile)
        w_tile = wbuf[:, :, :, cols].reshape(heads * HD, tile)
        proj_ref[:, :, cols] = (
            jnp.dot(att[...], w_tile, preferred_element_type=F32)
            .astype(BF16).reshape(2, rows, tile)
        )

    for j in range(nr):
        c_fwd(c_slot(j, 1 - y, k), c_rs.at[0], c_peer).wait_recv()
        c_fwd(c_slot(j, 1 - y, k), c_cs.at[2 * j + 1], c_peer).start()
    for j in range(nr):
        for yy in range(2):
            c_fwd(c_slot(j, yy, 1 - k), c_rs.at[0], c_peer).wait_recv()
    for j in range(nr):
        for q in range(4):
            i = j * 4 + q

            @pl.when(i != me)
            def _():
                rcopy(abuf.at[i], abuf.at[i], a_tx.at[i], a_rx.at[i], c_peer).wait_recv()

    def g_copy(zz):
        return rcopy(
            gbuf.at[zz], rbuf.at[z], g_tx.at[zz], g_rx.at[z], seq_id(zz, y, k)
        )

    lhs = jnp.concatenate([abuf[i] for i in range(grp)], axis=1)
    for cb in range(nc):
        rhs = cbuf[:, :, :, cb * cc:(cb + 1) * cc].reshape(grp * qn, cc)
        g_tile = jnp.dot(lhs, rhs, preferred_element_type=F32).astype(BF16)
        for rr in range(nz // nc):
            zz = rr * nc + cb
            gbuf[zz] = g_tile[rr * cr:(rr + 1) * cr]

            @pl.when(zz != z)
            def _():
                g_copy(zz).start()

            @pl.when(zz == z)
            def _():
                rbuf[zz] = g_tile[rr * cr:(rr + 1) * cr]

    total = jnp.zeros((cr, cc), F32)
    for zz in range(nz):
        @pl.when(zz != z)
        def _():
            rcopy(rbuf.at[zz], rbuf.at[zz], g_tx.at[zz], g_rx.at[zz], c_peer).wait_recv()

        total = total + rbuf[zz].astype(F32)

    def region(zz, yy, kk):
        return fbuf.at[seq_id(zz, yy, kk)]

    fbuf[s] = total.astype(BF16)

    def f_copy(zz, yy, kk, tx, peer):
        return rcopy(
            region(zz, yy, kk), region(zz, yy, kk), tx, f_rx.at[seq_id(zz, yy, kk)], peer
        )

    def f_z(zz):
        return f_copy(z, y, k, f_zs.at[zz], seq_id(zz, y, k))

    for zz in range(nz):
        @pl.when(zz != z)
        def _():
            f_z(zz).start()
    f_copy(z, y, k, f_ys.at[z], y_peer).start()
    f_copy(z, y, k, f_cs.at[2 * z + y], c_peer).start()
    for zz in range(nz):
        @pl.when(zz != z)
        def _():
            f_copy(zz, y, k, f_ys.at[zz], y_peer).wait_recv()
            f_copy(zz, y, k, f_ys.at[zz], y_peer).start()
            f_copy(zz, y, k, f_cs.at[2 * zz + y], c_peer).start()
    for zz in range(nz):
        f_copy(zz, 1 - y, k, f_cs.at[0], c_peer).wait_recv()
        f_copy(zz, 1 - y, k, f_cs.at[2 * zz + 1 - y], c_peer).start()
    for zz in range(nz):
        for yy in range(2):
            f_copy(zz, yy, 1 - k, f_cs.at[0], c_peer).wait_recv()

    for slot in range(ns):
        zz, q = slot // 4, slot % 4
        row = q * slice_rows + (zz // nc) * cr
        col = (zz % nc) * cc
        wg_ref[row:row + cr, col:col + cc] = fbuf[slot]

    @pl.loop(z + 1, nz)
    def _(zz):
        kv_z(zz).wait_send()

    @pl.when(z > 0)
    def _():
        kv_z(z - 1).wait_send()

    for zz in range(nz):
        @pl.when(zz <= z + 1)
        def _():
            kv_y(zz).wait_send()
            kv_c(zz, 0).wait_send()
            kv_c(zz, 1).wait_send()

    for step, i in noisy_steps:
        @pl.when(inside(step))
        def _():
            noisy_tx(step, i).wait_send()
    noisy_c(own_noisy, 1, 2).wait_send()
    noisy_relay(True)
    for j in range(nr):
        @pl.when(j != r)
        def _():
            c_rep(j).wait_send()
            w_rep(j).wait_send()
            w_fwd(j, k, w_cs.at[j]).wait_send()
        c_fwd(c_slot(j, y, k), c_ys.at[j], y_peer).wait_send()
        for h in range(2):
            c_fwd(c_slot(j, h, k), c_cs.at[2 * j + h], c_peer).wait_send()
        for q in range(4):
            @pl.when(j * 4 + q != me)
            def _():
                a_copy(j, q).wait_send()
    for zz in range(nz):
        @pl.when(zz != z)
        def _():
            g_copy(zz).wait_send()
            f_z(zz).wait_send()
        f_copy(zz, y, k, f_ys.at[zz], y_peer).wait_send()
        for yy in range(2):
            f_copy(zz, yy, k, f_cs.at[2 * zz + yy], c_peer).wait_send()


def on_device(queries, keys_values, block_lengths, out_weight, cotangent):
    ns, nr = lax.axis_size("seq"), lax.axis_size("rep")
    nz = ns // 4
    rows, q_width = queries.shape[2], queries.shape[3]
    kv_width = keys_values.shape[4]
    w_rows, out_width = out_weight.shape
    kvh, gs = kv_width // HD, q_width // kv_width
    qn = 2 * rows
    lanes = gs * qn
    slice_rows = w_rows // 4
    nc = min(nz, out_width // 128)
    cr, cc = slice_rows // (nz // nc), out_width // nc
    dma = pltpu.SemaphoreType.DMA
    vmem, hbm = pl.BlockSpec(memory_space=pltpu.VMEM), pl.BlockSpec(memory_space=pl.ANY)
    projected, grad = pl.pallas_call(
        functools.partial(kernel, ns, nr, nc),
        out_shape=(
            jax.ShapeDtypeStruct((2, rows, out_width), BF16),
            jax.ShapeDtypeStruct((w_rows, out_width), BF16),
        ),
        in_specs=[pl.BlockSpec(memory_space=pltpu.SMEM), vmem, hbm, hbm, hbm],
        out_specs=(vmem, vmem),
        scratch_shapes=[
            pltpu.VMEM((ns, 2, rows, kv_width), BF16),
            pltpu.VMEM((5, 2, rows, kv_width), BF16),
            pltpu.VMEM((nr, 2, w_rows // 2, out_width), BF16),
            pltpu.VMEM((4 * nr, 2, rows, out_width), BF16),
            pltpu.VMEM((4 * nr, slice_rows, qn), BF16),
            pltpu.VMEM((q_width, qn), BF16),
            pltpu.VMEM((qn, q_width), BF16),
            pltpu.VMEM((kvh, HD, lanes), F32),
            pltpu.VMEM((kvh, 1, lanes), F32),
            pltpu.VMEM((kvh, 1, lanes), F32),
            pltpu.VMEM((nz, cr, cc), BF16),
            pltpu.VMEM((nz, cr, cc), BF16),
            pltpu.VMEM((ns, cr, cc), BF16),
            dma((5,)),
            dma((ns,)), dma((nz,)), dma((nz,)), dma((ns // 2,)),
            dma((5,)), dma((4,)),
            dma((nr, 2)), dma((nr,)), dma((nr,)),
            dma((4 * nr,)), dma((nr,)), dma((nr,)), dma((2 * nr,)),
            dma((4 * nr,)), dma((4 * nr,)),
            dma((nz,)), dma((nz,)),
            dma((ns,)), dma((nz,)), dma((nz,)), dma((ns // 2,)),
        ],
        compiler_params=pltpu.CompilerParams(
            collective_id=0, has_side_effects=True, vmem_limit_bytes=60 * 2**20
        ),
    )(block_lengths, queries[0], keys_values, out_weight, cotangent)
    return projected[None], grad.astype(F32)


def solution(mesh):
    placed = (
        P("rep", None, "seq", None),
        P("rep", None, None, "seq", None),
        P("rep", None),
        P("rep", None),
        P("rep", None, "seq", None),
    )
    return jax.shard_map(
        on_device,
        mesh=mesh,
        in_specs=placed,
        out_specs=(P("rep", None, "seq", None), P("rep", None)),
        check_vma=False,
    )
```

```python
import functools
import math

import jax
import jax.numpy as jnp
from jax import lax
from jax.experimental import pallas as pl
from jax.experimental.pallas import tpu as pltpu
from jax.sharding import PartitionSpec as P

HD = 128
NEG = -1e30
MESH = pl.DeviceIdType.MESH
F32 = jnp.float32
BF16 = jnp.bfloat16


def kernel(
    ns, nr, nc,
    len_ref, q_ref, kv_ref, w_ref, cot_ref,
    proj_ref, wg_ref,
    kvc, kvn, wbuf, cbuf, abuf, att_t, att, acc, m_ref, l_ref, gbuf, rbuf, fbuf,
    loc, kv_rx, kv_zs, kv_ws, kv_ys, kv_cs, n_rx, n_tx, w_rx, w_tx, w_cs,
    c_rx, c_rs, c_ys, c_cs, a_rx, a_tx, g_rx, g_tx, f_rx, f_zs, f_ys, f_cs,
):
    nz = ns // 4
    grp = 4 * nr
    rows = q_ref.shape[1]
    qn = 2 * rows
    heads = q_ref.shape[2] // HD
    kvh = kv_ref.shape[4] // HD
    gs = heads // kvh
    lanes = gs * qn
    nblk = len_ref.shape[1]
    slice_rows = abuf.shape[1]
    cr, cc = gbuf.shape[1], gbuf.shape[2]
    w_half = wbuf.shape[2]

    s = lax.axis_index("seq")
    r = lax.axis_index("rep")
    k = lax.rem(s, 2)
    y = lax.rem(s // 2, 2)
    z = s // 4
    base = 4 * z
    y_peer = base + 2 * (1 - y) + k
    c_peer = base + 2 * y + 1 - k

    def seq_id(zz, yy, kk):
        return 4 * zz + 2 * yy + kk

    def rcopy(src, dst, tx, rx, seq, rep=None):
        return pltpu.make_async_remote_copy(
            src_ref=src, dst_ref=dst, send_sem=tx, recv_sem=rx,
            device_id=(seq, r if rep is None else rep), device_id_type=MESH,
        )

    barrier = pltpu.get_barrier_semaphore()

    @pl.loop(0, ns)
    def _(i):
        @pl.when(i != s)
        def _():
            pl.semaphore_signal(barrier, inc=1, device_id=(i, r), device_id_type=MESH)

    for j in range(nr):
        @pl.when(j != r)
        def _():
            for q in range(4):
                pl.semaphore_signal(
                    barrier, inc=1, device_id=(base + q, j), device_id_type=MESH
                )

    own_kv = pltpu.make_async_copy(kv_ref.at[0, 1], kvc.at[s], loc.at[0])
    own_n = pltpu.make_async_copy(kv_ref.at[0, 0], kvn.at[2], loc.at[1])
    own_w = [
        pltpu.make_async_copy(
            w_ref.at[pl.ds(h * w_half, w_half)], wbuf.at[r, h], loc.at[2 + h]
        )
        for h in range(2)
    ]
    me = r * 4 + 2 * y + k
    own_c = pltpu.make_async_copy(cot_ref.at[0], cbuf.at[me], loc.at[4])
    for cp in [own_kv, own_n, own_c] + own_w:
        cp.start()

    pl.semaphore_wait(barrier, ns - 1 + 4 * (nr - 1))

    clean = kv_ref.at[0, 1]

    def kv_z(zz):
        return rcopy(clean, kvc.at[s], kv_zs.at[zz], kv_rx.at[s], seq_id(zz, y, k))

    def kv_y(zz):
        slot = seq_id(zz, y, k)
        return rcopy(kvc.at[slot], kvc.at[slot], kv_ys.at[zz], kv_rx.at[slot], y_peer)

    def kv_c(zz, yy):
        slot = seq_id(zz, yy, k)
        return rcopy(
            kvc.at[slot], kvc.at[slot], kv_cs.at[2 * zz + yy], kv_rx.at[slot], c_peer
        )

    def kv_wait(zz, yy, kk):
        slot = seq_id(zz, yy, kk)
        rcopy(kvc.at[slot], kvc.at[slot], kv_zs.at[0], kv_rx.at[slot], c_peer).wait_recv()

    kv_own_y = rcopy(clean, kvc.at[s], kv_ys.at[z], kv_rx.at[s], y_peer)
    kv_own_c = rcopy(clean, kvc.at[s], kv_cs.at[2 * z + y], kv_rx.at[s], c_peer)

    @pl.loop(z + 1, nz)
    def _(zz):
        kv_z(zz).start()

    kv_own_y.start()
    kv_own_c.start()

    @pl.when(z > 0)
    def _():
        kv_z(z - 1).start()

    noisy_steps = ((2, 0), (-2, 1))
    own_noisy = kv_ref.at[0, 0]

    def inside(step):
        return (s + step >= 0) & (s + step < ns)

    def noisy_tx(step, i):
        return rcopy(own_noisy, kvn.at[2 - step], n_tx.at[i], n_rx.at[2 - step], s + step)

    def noisy_c(src, slot, i):
        return rcopy(src, kvn.at[slot], n_tx.at[i], n_rx.at[slot], c_peer)

    def noisy_wait(slot):
        rcopy(kvn.at[slot], kvn.at[slot], n_tx.at[0], n_rx.at[slot], c_peer).wait_recv()

    for step, i in noisy_steps:
        @pl.when(inside(step))
        def _():
            noisy_tx(step, i).start()

        @pl.when(jnp.logical_not(inside(step)))
        def _():
            kvn[2 + step] = jnp.zeros(kvn.shape[1:], kvn.dtype)

    @pl.when(k == 0)
    def _():
        noisy_c(own_noisy, 1, 2).start()

    @pl.when(k == 1)
    def _():
        noisy_c(own_noisy, 3, 2).start()

    @pl.when((k == 0) & (s == 0))
    def _():
        kvn[1] = jnp.zeros(kvn.shape[1:], kvn.dtype)

    @pl.when((k == 1) & (s == ns - 1))
    def _():
        kvn[3] = jnp.zeros(kvn.shape[1:], kvn.dtype)

    def noisy_relay(finish):
        for kk, step, slot in ((0, 2, 3), (1, -2, 1)):
            @pl.when((k == kk) & inside(step))
            def _():
                copy = noisy_c(kvn.at[2 + step], slot, 3)
                if finish:
                    copy.wait_send()
                else:
                    noisy_wait(2 + step)
                    copy.start()

    def c_rep(j):
        return rcopy(cot_ref.at[0], cbuf.at[me], c_rs.at[j], c_rx.at[me], s, j)

    def w_rep(j):
        return rcopy(
            w_ref.at[pl.ds(pl.multiple_of(k * w_half, w_half), w_half)],
            wbuf.at[r, k], w_tx.at[j], w_rx.at[r, k], s, j,
        )

    for j in range(nr):
        @pl.when(j != r)
        def _():
            c_rep(j).start()
            w_rep(j).start()

    lane = lax.broadcasted_iota(jnp.int32, (1, lanes), 1)
    qi = lax.rem(lane, qn)
    noisy = qi < rows
    qpos = s * rows + lax.rem(qi, rows)

    def find(b, carry):
        prev, start, end = carry
        stop = prev + len_ref[0, b]
        hit = (qpos >= prev) & (qpos < stop)
        return stop, jnp.where(hit, prev, start), jnp.where(hit, stop, end)

    zero_row = jnp.zeros((1, lanes), jnp.int32)
    _, start, end = lax.fori_loop(0, nblk, find, (jnp.int32(0), zero_row, zero_row))
    clean_hi = jnp.where(noisy, start, end)
    noisy_lo = jnp.where(noisy, start, 0)
    noisy_hi = jnp.where(noisy, end, 0)

    m_ref[...] = jnp.full(m_ref.shape, NEG, F32)
    l_ref[...] = jnp.zeros(l_ref.shape, F32)
    acc[...] = jnp.zeros(acc.shape, F32)
    score_scale = math.log2(math.e) / math.sqrt(HD)

    def absorb(load, allowed):
        for g in range(kvh):
            keys = load(0, g)
            vals = load(1, g)
            qg = jnp.concatenate(
                [
                    q_ref[:, :, (g * gs + j) * HD:(g * gs + j + 1) * HD].reshape(qn, HD)
                    for j in range(gs)
                ],
                axis=0,
            )
            sc = lax.dot_general(
                keys, qg, (((1,), (1,)), ((), ())), preferred_element_type=F32
            )
            sc = jnp.where(allowed, sc * score_scale, NEG)
            m_old = m_ref[g]
            m_new = jnp.maximum(m_old, jnp.max(sc, axis=0, keepdims=True))
            m_use = jnp.maximum(m_new, NEG / 2)
            p = jnp.exp2(sc - m_use)
            f = jnp.exp2(m_old - m_use)
            m_ref[g] = m_new
            l_ref[g] = l_ref[g] * f + jnp.sum(p, axis=0, keepdims=True)
            up = lax.dot_general(
                vals, p.astype(BF16), (((0,), (0,)), ((), ())), preferred_element_type=F32
            )
            acc[g] = acc[g] * f + up

    kp_n = (s - 2) * rows + lax.broadcasted_iota(jnp.int32, (5 * rows, lanes), 0)

    def noisy_absorb():
        own_n.wait()

        for kk, step in ((0, -2), (1, 2)):
            @pl.when((k == kk) & inside(step))
            def _():
                noisy_wait(2 + step)

        for slot, kk, edge in ((1, 0, 0), (3, 1, ns - 1)):
            @pl.when((k == 1 - kk) | (s != edge))
            def _():
                noisy_wait(slot)

        absorb(
            lambda a, g: kvn[:, a, :, g * HD:(g + 1) * HD].reshape(5 * rows, HD),
            (kp_n >= noisy_lo) & (kp_n < noisy_hi),
        )

    def c_slot(j, yy, kk):
        return j * 4 + 2 * yy + kk

    def c_fwd(slot, tx, peer):
        return rcopy(cbuf.at[slot], cbuf.at[slot], tx, c_rx.at[slot], peer)

    def kv_wide(zz):
        slot = seq_id(0, 1 - y, k)
        return rcopy(
            kvc.at[slot], kvc.at[slot], kv_ws.at[zz], kv_rx.at[slot], seq_id(zz, y, k)
        )

    own_kv.wait()

    @pl.when(z == 0)
    def _():
        kv_wait(0, 1 - y, k)
        for zz in range(nz - 1, 0, -1):
            kv_wide(zz).start()
        kv_c(0, 1 - y).start()
    order = list(range(nz - 1, -1, -1))
    for i in range(nz + 2):
        if i < nz:
            zz = order[i]

            @pl.when((zz <= z + 1) & (zz != z))
            def _():
                kv_wait(zz, y, k)
                if zz > 0:
                    kv_y(zz).start()
                kv_c(zz, y).start()

        if i == nz - 1:
            own_c.wait()
            for j in range(nr):
                @pl.when(j != r)
                def _():
                    c_fwd(c_slot(j, y, k), c_rs.at[j], c_peer).wait_recv()
                c_fwd(c_slot(j, y, k), c_ys.at[j], y_peer).start()

        if 1 <= i <= nz:
            zz = order[i - 1]

            @pl.when((zz <= z + 1) & ((zz > 0) | (z > 0)))
            def _():
                kv_wait(zz, 1 - y, k)
                kv_c(zz, 1 - y).start()

        if i == nz - 1:
            noisy_relay(False)

        if i == nz:
            for j in range(nr):
                c_fwd(c_slot(j, y, k), c_cs.at[2 * j], c_peer).start()
            noisy_absorb()

        if i >= 2:
            zz = order[i - 2]

            @pl.when(zz <= z + 1)
            def _():
                kv_wait(zz, y, 1 - k)
                kv_wait(zz, 1 - y, 1 - k)
                kp = zz * (4 * rows) + lax.broadcasted_iota(
                    jnp.int32, (4 * rows, lanes), 0
                )
                absorb(
                    lambda a, g: kvc[4 * zz:4 * zz + 4, a, :, g * HD:(g + 1) * HD].reshape(
                        4 * rows, HD
                    ),
                    kp < clean_hi,
                )

    for g in range(kvh):
        o = acc[g] / l_ref[g]
        for j in range(gs):
            h = g * gs + j
            part = o[:, j * qn:(j + 1) * qn]
            att_t[h * HD:(h + 1) * HD, :] = part.astype(BF16)
            att[:, h * HD:(h + 1) * HD] = part.T.astype(BF16)

    def a_copy(j, q):
        i = j * 4 + q
        return rcopy(
            att_t.at[pl.ds(i * slice_rows, slice_rows)], abuf.at[me], a_tx.at[i],
            a_rx.at[me], base + q, j,
        )

    for j in range(nr):
        for q in range(4):
            i = j * 4 + q

            @pl.when(i != me)
            def _():
                a_copy(j, q).start()

    abuf[me] = att_t[pl.ds(pl.multiple_of(me * slice_rows, slice_rows), slice_rows), :]

    for cp in own_w:
        cp.wait()

    def w_fwd(j, h, tx):
        return rcopy(wbuf.at[j, h], wbuf.at[j, h], tx, w_rx.at[j, h], c_peer)

    for j in range(nr):
        @pl.when(j != r)
        def _():
            w_fwd(j, k, w_tx.at[j]).wait_recv()
            w_fwd(j, k, w_cs.at[j]).start()
    for j in range(nr):
        @pl.when(j != r)
        def _():
            w_fwd(j, 1 - k, w_tx.at[j]).wait_recv()

    tile = 256
    for t in range(wbuf.shape[3] // tile):
        cols = slice(t * tile, (t + 1) * tile)
        w_tile = wbuf[:, :, :, cols].reshape(heads * HD, tile)
        proj_ref[:, :, cols] = (
            jnp.dot(att[...], w_tile, preferred_element_type=F32)
            .astype(BF16).reshape(2, rows, tile)
        )

    for j in range(nr):
        c_fwd(c_slot(j, 1 - y, k), c_rs.at[0], c_peer).wait_recv()
        c_fwd(c_slot(j, 1 - y, k), c_cs.at[2 * j + 1], c_peer).start()
    for j in range(nr):
        for yy in range(2):
            c_fwd(c_slot(j, yy, 1 - k), c_rs.at[0], c_peer).wait_recv()
    for j in range(nr):
        for q in range(4):
            i = j * 4 + q

            @pl.when(i != me)
            def _():
                rcopy(abuf.at[i], abuf.at[i], a_tx.at[i], a_rx.at[i], c_peer).wait_recv()

    def g_copy(zz):
        return rcopy(
            gbuf.at[zz], rbuf.at[z], g_tx.at[zz], g_rx.at[z], seq_id(zz, y, k)
        )

    lhs = jnp.concatenate([abuf[i] for i in range(grp)], axis=1)
    for cb in range(nc):
        rhs = cbuf[:, :, :, cb * cc:(cb + 1) * cc].reshape(grp * qn, cc)
        g_tile = jnp.dot(lhs, rhs, preferred_element_type=F32).astype(BF16)
        for rr in range(nz // nc):
            zz = rr * nc + cb
            gbuf[zz] = g_tile[rr * cr:(rr + 1) * cr]

            @pl.when(zz != z)
            def _():
                g_copy(zz).start()

            @pl.when(zz == z)
            def _():
                rbuf[zz] = g_tile[rr * cr:(rr + 1) * cr]

    total = jnp.zeros((cr, cc), F32)
    for zz in range(nz):
        @pl.when(zz != z)
        def _():
            rcopy(rbuf.at[zz], rbuf.at[zz], g_tx.at[zz], g_rx.at[zz], c_peer).wait_recv()

        total = total + rbuf[zz].astype(F32)

    def region(zz, yy, kk):
        return fbuf.at[seq_id(zz, yy, kk)]

    fbuf[s] = total.astype(BF16)

    def f_copy(zz, yy, kk, tx, peer):
        return rcopy(
            region(zz, yy, kk), region(zz, yy, kk), tx, f_rx.at[seq_id(zz, yy, kk)], peer
        )

    def f_z(zz):
        return f_copy(z, y, k, f_zs.at[zz], seq_id(zz, y, k))

    for zz in range(nz):
        @pl.when(zz != z)
        def _():
            f_z(zz).start()
    f_copy(z, y, k, f_ys.at[z], y_peer).start()
    f_copy(z, y, k, f_cs.at[2 * z + y], c_peer).start()
    for zz in range(nz):
        @pl.when(zz != z)
        def _():
            f_copy(zz, y, k, f_ys.at[zz], y_peer).wait_recv()
            f_copy(zz, y, k, f_ys.at[zz], y_peer).start()
            f_copy(zz, y, k, f_cs.at[2 * zz + y], c_peer).start()
    for zz in range(nz):
        f_copy(zz, 1 - y, k, f_cs.at[0], c_peer).wait_recv()
        f_copy(zz, 1 - y, k, f_cs.at[2 * zz + 1 - y], c_peer).start()
    for zz in range(nz):
        for yy in range(2):
            f_copy(zz, yy, 1 - k, f_cs.at[0], c_peer).wait_recv()

    for slot in range(ns):
        zz, q = slot // 4, slot % 4
        row = q * slice_rows + (zz // nc) * cr
        col = (zz % nc) * cc
        wg_ref[row:row + cr, col:col + cc] = fbuf[slot]

    @pl.loop(z + 1, nz)
    def _(zz):
        kv_z(zz).wait_send()

    @pl.when(z > 0)
    def _():
        kv_z(z - 1).wait_send()

    for zz in range(nz):
        @pl.when(zz <= z + 1)
        def _():
            if zz > 0:
                kv_y(zz).wait_send()
            kv_c(zz, 0).wait_send()
            kv_c(zz, 1).wait_send()

    @pl.when(z == 0)
    def _():
        kv_y(0).wait_send()
        for zz in range(1, nz):
            kv_wide(zz).wait_send()

    for step, i in noisy_steps:
        @pl.when(inside(step))
        def _():
            noisy_tx(step, i).wait_send()
    noisy_c(own_noisy, 1, 2).wait_send()
    noisy_relay(True)
    for j in range(nr):
        @pl.when(j != r)
        def _():
            c_rep(j).wait_send()
            w_rep(j).wait_send()
            w_fwd(j, k, w_cs.at[j]).wait_send()
        c_fwd(c_slot(j, y, k), c_ys.at[j], y_peer).wait_send()
        for h in range(2):
            c_fwd(c_slot(j, h, k), c_cs.at[2 * j + h], c_peer).wait_send()
        for q in range(4):
            @pl.when(j * 4 + q != me)
            def _():
                a_copy(j, q).wait_send()
    for zz in range(nz):
        @pl.when(zz != z)
        def _():
            g_copy(zz).wait_send()
            f_z(zz).wait_send()
        f_copy(zz, y, k, f_ys.at[zz], y_peer).wait_send()
        for yy in range(2):
            f_copy(zz, yy, k, f_cs.at[2 * zz + yy], c_peer).wait_send()


def on_device(queries, keys_values, block_lengths, out_weight, cotangent):
    ns, nr = lax.axis_size("seq"), lax.axis_size("rep")
    nz = ns // 4
    rows, q_width = queries.shape[2], queries.shape[3]
    kv_width = keys_values.shape[4]
    w_rows, out_width = out_weight.shape
    kvh, gs = kv_width // HD, q_width // kv_width
    qn = 2 * rows
    lanes = gs * qn
    slice_rows = w_rows // 4
    nc = min(nz, out_width // 128)
    cr, cc = slice_rows // (nz // nc), out_width // nc
    dma = pltpu.SemaphoreType.DMA
    vmem, hbm = pl.BlockSpec(memory_space=pltpu.VMEM), pl.BlockSpec(memory_space=pl.ANY)
    projected, grad = pl.pallas_call(
        functools.partial(kernel, ns, nr, nc),
        out_shape=(
            jax.ShapeDtypeStruct((2, rows, out_width), BF16),
            jax.ShapeDtypeStruct((w_rows, out_width), BF16),
        ),
        in_specs=[pl.BlockSpec(memory_space=pltpu.SMEM), vmem, hbm, hbm, hbm],
        out_specs=(vmem, vmem),
        scratch_shapes=[
            pltpu.VMEM((ns, 2, rows, kv_width), BF16),
            pltpu.VMEM((5, 2, rows, kv_width), BF16),
            pltpu.VMEM((nr, 2, w_rows // 2, out_width), BF16),
            pltpu.VMEM((4 * nr, 2, rows, out_width), BF16),
            pltpu.VMEM((4 * nr, slice_rows, qn), BF16),
            pltpu.VMEM((q_width, qn), BF16),
            pltpu.VMEM((qn, q_width), BF16),
            pltpu.VMEM((kvh, HD, lanes), F32),
            pltpu.VMEM((kvh, 1, lanes), F32),
            pltpu.VMEM((kvh, 1, lanes), F32),
            pltpu.VMEM((nz, cr, cc), BF16),
            pltpu.VMEM((nz, cr, cc), BF16),
            pltpu.VMEM((ns, cr, cc), BF16),
            dma((5,)),
            dma((ns,)), dma((nz,)), dma((nz,)), dma((nz,)), dma((ns // 2,)),
            dma((5,)), dma((4,)),
            dma((nr, 2)), dma((nr,)), dma((nr,)),
            dma((4 * nr,)), dma((nr,)), dma((nr,)), dma((2 * nr,)),
            dma((4 * nr,)), dma((4 * nr,)),
            dma((nz,)), dma((nz,)),
            dma((ns,)), dma((nz,)), dma((nz,)), dma((ns // 2,)),
        ],
        compiler_params=pltpu.CompilerParams(
            collective_id=0, has_side_effects=True, vmem_limit_bytes=60 * 2**20
        ),
    )(block_lengths, queries[0], keys_values, out_weight, cotangent)
    return projected[None], grad.astype(F32)


def solution(mesh):
    placed = (
        P("rep", None, "seq", None),
        P("rep", None, None, "seq", None),
        P("rep", None),
        P("rep", None),
        P("rep", None, "seq", None),
    )
    return jax.shard_map(
        on_device,
        mesh=mesh,
        in_specs=placed,
        out_specs=(P("rep", None, "seq", None), P("rep", None)),
        check_vma=False,
    )
```

```python
import functools
import math

import jax
import jax.numpy as jnp
from jax import lax
from jax.experimental import pallas as pl
from jax.experimental.pallas import tpu as pltpu
from jax.sharding import PartitionSpec as P

HD = 128
NEG = -1e30
MESH = pl.DeviceIdType.MESH
F32 = jnp.float32
BF16 = jnp.bfloat16


def kernel(
    ns, nr, nc,
    len_ref, q_ref, kv_ref, w_ref, cot_ref,
    proj_ref, wg_ref,
    kvc, kvn, wbuf, cbuf, abuf, att_t, att, acc, m_ref, l_ref, gbuf, rbuf, fbuf,
    loc, kv_rx, kv_zs, kv_ys, kv_cs, n_rx, n_tx, w_rx, w_tx, w_cs,
    c_rx, c_rs, c_ys, c_cs, a_rx, a_tx, g_rx, g_tx, f_rx, f_zs, f_ys, f_cs,
):
    nz = ns // 4
    grp = 4 * nr
    rows = q_ref.shape[1]
    qn = 2 * rows
    heads = q_ref.shape[2] // HD
    kvh = kv_ref.shape[4] // HD
    gs = heads // kvh
    lanes = gs * qn
    nblk = len_ref.shape[1]
    slice_rows = abuf.shape[1]
    cr, cc = gbuf.shape[1], gbuf.shape[2]
    w_half = wbuf.shape[2]

    s = lax.axis_index("seq")
    r = lax.axis_index("rep")
    k = lax.rem(s, 2)
    y = lax.rem(s // 2, 2)
    z = s // 4
    base = 4 * z
    y_peer = base + 2 * (1 - y) + k
    c_peer = base + 2 * y + 1 - k

    def seq_id(zz, yy, kk):
        return 4 * zz + 2 * yy + kk

    def rcopy(src, dst, tx, rx, seq, rep=None):
        return pltpu.make_async_remote_copy(
            src_ref=src, dst_ref=dst, send_sem=tx, recv_sem=rx,
            device_id=(seq, r if rep is None else rep), device_id_type=MESH,
        )

    barrier = pltpu.get_barrier_semaphore()

    @pl.loop(0, ns)
    def _(i):
        @pl.when(i != s)
        def _():
            pl.semaphore_signal(barrier, inc=1, device_id=(i, r), device_id_type=MESH)

    for j in range(nr):
        @pl.when(j != r)
        def _():
            for q in range(4):
                pl.semaphore_signal(
                    barrier, inc=1, device_id=(base + q, j), device_id_type=MESH
                )

    own_kv = pltpu.make_async_copy(kv_ref.at[0, 1], kvc.at[s], loc.at[0])
    own_n = pltpu.make_async_copy(kv_ref.at[0, 0], kvn.at[2], loc.at[1])
    own_w = [
        pltpu.make_async_copy(
            w_ref.at[pl.ds(h * w_half, w_half)], wbuf.at[r, h], loc.at[2 + h]
        )
        for h in range(2)
    ]
    me = r * 4 + 2 * y + k
    own_c = pltpu.make_async_copy(cot_ref.at[0], cbuf.at[me], loc.at[4])
    for cp in [own_kv, own_n, own_c] + own_w:
        cp.start()

    pl.semaphore_wait(barrier, ns - 1 + 4 * (nr - 1))

    clean = kv_ref.at[0, 1]

    def kv_z(zz):
        return rcopy(clean, kvc.at[s], kv_zs.at[zz], kv_rx.at[s], seq_id(zz, y, k))

    def kv_y(zz):
        slot = seq_id(zz, y, k)
        return rcopy(kvc.at[slot], kvc.at[slot], kv_ys.at[zz], kv_rx.at[slot], y_peer)

    def kv_c(zz, yy):
        slot = seq_id(zz, yy, k)
        return rcopy(
            kvc.at[slot], kvc.at[slot], kv_cs.at[2 * zz + yy], kv_rx.at[slot], c_peer
        )

    def kv_wait(zz, yy, kk):
        slot = seq_id(zz, yy, kk)
        rcopy(kvc.at[slot], kvc.at[slot], kv_zs.at[0], kv_rx.at[slot], c_peer).wait_recv()

    kv_own_y = rcopy(clean, kvc.at[s], kv_ys.at[z], kv_rx.at[s], y_peer)
    kv_own_c = rcopy(clean, kvc.at[s], kv_cs.at[2 * z + y], kv_rx.at[s], c_peer)

    @pl.loop(z + 1, nz)
    def _(zz):
        kv_z(zz).start()

    kv_own_y.start()
    kv_own_c.start()

    @pl.when(z > 0)
    def _():
        kv_z(z - 1).start()

    noisy_steps = ((2, 0), (-2, 1))
    own_noisy = kv_ref.at[0, 0]

    def inside(step):
        return (s + step >= 0) & (s + step < ns)

    def noisy_tx(step, i):
        return rcopy(own_noisy, kvn.at[2 - step], n_tx.at[i], n_rx.at[2 - step], s + step)

    def noisy_c(src, slot, i):
        return rcopy(src, kvn.at[slot], n_tx.at[i], n_rx.at[slot], c_peer)

    def noisy_wait(slot):
        rcopy(kvn.at[slot], kvn.at[slot], n_tx.at[0], n_rx.at[slot], c_peer).wait_recv()

    for step, i in noisy_steps:
        @pl.when(inside(step))
        def _():
            noisy_tx(step, i).start()

        @pl.when(jnp.logical_not(inside(step)))
        def _():
            kvn[2 + step] = jnp.zeros(kvn.shape[1:], kvn.dtype)

    @pl.when(k == 0)
    def _():
        noisy_c(own_noisy, 1, 2).start()

    @pl.when(k == 1)
    def _():
        noisy_c(own_noisy, 3, 2).start()

    @pl.when((k == 0) & (s == 0))
    def _():
        kvn[1] = jnp.zeros(kvn.shape[1:], kvn.dtype)

    @pl.when((k == 1) & (s == ns - 1))
    def _():
        kvn[3] = jnp.zeros(kvn.shape[1:], kvn.dtype)

    def noisy_relay(finish):
        for kk, step, slot in ((0, 2, 3), (1, -2, 1)):
            @pl.when((k == kk) & inside(step))
            def _():
                copy = noisy_c(kvn.at[2 + step], slot, 3)
                if finish:
                    copy.wait_send()
                else:
                    noisy_wait(2 + step)
                    copy.start()

    def c_rep(j):
        return rcopy(cot_ref.at[0], cbuf.at[me], c_rs.at[j], c_rx.at[me], s, j)

    def w_rep(j):
        return rcopy(
            w_ref.at[pl.ds(pl.multiple_of(k * w_half, w_half), w_half)],
            wbuf.at[r, k], w_tx.at[j], w_rx.at[r, k], s, j,
        )

    for j in range(nr):
        @pl.when(j != r)
        def _():
            c_rep(j).start()
            w_rep(j).start()

    lane = lax.broadcasted_iota(jnp.int32, (1, lanes), 1)
    qi = lax.rem(lane, qn)
    noisy = qi < rows
    qpos = s * rows + lax.rem(qi, rows)

    def find(b, carry):
        prev, start, end = carry
        stop = prev + len_ref[0, b]
        hit = (qpos >= prev) & (qpos < stop)
        return stop, jnp.where(hit, prev, start), jnp.where(hit, stop, end)

    zero_row = jnp.zeros((1, lanes), jnp.int32)
    _, start, end = lax.fori_loop(0, nblk, find, (jnp.int32(0), zero_row, zero_row))
    clean_hi = jnp.where(noisy, start, end)
    noisy_lo = jnp.where(noisy, start, 0)
    noisy_hi = jnp.where(noisy, end, 0)

    m_ref[...] = jnp.full(m_ref.shape, NEG, F32)
    l_ref[...] = jnp.zeros(l_ref.shape, F32)
    acc[...] = jnp.zeros(acc.shape, F32)
    score_scale = math.log2(math.e) / math.sqrt(HD)

    def absorb(load, allowed):
        for g in range(kvh):
            keys = load(0, g)
            vals = load(1, g)
            qg = jnp.concatenate(
                [
                    q_ref[:, :, (g * gs + j) * HD:(g * gs + j + 1) * HD].reshape(qn, HD)
                    for j in range(gs)
                ],
                axis=0,
            )
            sc = lax.dot_general(
                keys, qg, (((1,), (1,)), ((), ())), preferred_element_type=F32
            )
            sc = jnp.where(allowed, sc * score_scale, NEG)
            m_old = m_ref[g]
            m_new = jnp.maximum(m_old, jnp.max(sc, axis=0, keepdims=True))
            m_use = jnp.maximum(m_new, NEG / 2)
            p = jnp.exp2(sc - m_use)
            f = jnp.exp2(m_old - m_use)
            m_ref[g] = m_new
            l_ref[g] = l_ref[g] * f + jnp.sum(p, axis=0, keepdims=True)
            up = lax.dot_general(
                vals, p.astype(BF16), (((0,), (0,)), ((), ())), preferred_element_type=F32
            )
            acc[g] = acc[g] * f + up

    kp_n = (s - 2) * rows + lax.broadcasted_iota(jnp.int32, (5 * rows, lanes), 0)

    def noisy_absorb():
        own_n.wait()

        for kk, step in ((0, -2), (1, 2)):
            @pl.when((k == kk) & inside(step))
            def _():
                noisy_wait(2 + step)

        for slot, kk, edge in ((1, 0, 0), (3, 1, ns - 1)):
            @pl.when((k == 1 - kk) | (s != edge))
            def _():
                noisy_wait(slot)

        absorb(
            lambda a, g: kvn[:, a, :, g * HD:(g + 1) * HD].reshape(5 * rows, HD),
            (kp_n >= noisy_lo) & (kp_n < noisy_hi),
        )

    def c_slot(j, yy, kk):
        return j * 4 + 2 * yy + kk

    def c_fwd(slot, tx, peer):
        return rcopy(cbuf.at[slot], cbuf.at[slot], tx, c_rx.at[slot], peer)

    own_kv.wait()
    own_c.wait()
    c_fwd(me, c_ys.at[r], y_peer).start()
    order = list(range(nz - 1, -1, -1))
    for i in range(nz + 2):
        if i < nz:
            zz = order[i]

            @pl.when((zz <= z + 1) & (zz != z))
            def _():
                kv_wait(zz, y, k)
                kv_y(zz).start()
                kv_c(zz, y).start()

        if i == nz - 1:
            for j in range(nr):
                @pl.when(j != r)
                def _():
                    c_fwd(c_slot(j, y, k), c_rs.at[j], c_peer).wait_recv()
                    c_fwd(c_slot(j, y, k), c_ys.at[j], y_peer).start()

        if 1 <= i <= nz:
            zz = order[i - 1]

            @pl.when(zz <= z + 1)
            def _():
                kv_wait(zz, 1 - y, k)
                kv_c(zz, 1 - y).start()

        if i == nz - 1:
            noisy_relay(False)

        if i == nz:
            for j in range(nr):
                c_fwd(c_slot(j, y, k), c_cs.at[2 * j], c_peer).start()
            noisy_absorb()

        if i >= 2:
            zz = order[i - 2]

            @pl.when(zz <= z + 1)
            def _():
                kv_wait(zz, y, 1 - k)
                kv_wait(zz, 1 - y, 1 - k)
                kp = zz * (4 * rows) + lax.broadcasted_iota(
                    jnp.int32, (4 * rows, lanes), 0
                )
                absorb(
                    lambda a, g: kvc[4 * zz:4 * zz + 4, a, :, g * HD:(g + 1) * HD].reshape(
                        4 * rows, HD
                    ),
                    kp < clean_hi,
                )

    for g in range(kvh):
        o = acc[g] / l_ref[g]
        for j in range(gs):
            h = g * gs + j
            part = o[:, j * qn:(j + 1) * qn]
            att_t[h * HD:(h + 1) * HD, :] = part.astype(BF16)
            att[:, h * HD:(h + 1) * HD] = part.T.astype(BF16)

    def a_copy(j, q):
        i = j * 4 + q
        return rcopy(
            att_t.at[pl.ds(i * slice_rows, slice_rows)], abuf.at[me], a_tx.at[i],
            a_rx.at[me], base + q, j,
        )

    for j in range(nr):
        for q in range(4):
            i = j * 4 + q

            @pl.when(i != me)
            def _():
                a_copy(j, q).start()

    abuf[me] = att_t[pl.ds(pl.multiple_of(me * slice_rows, slice_rows), slice_rows), :]

    for cp in own_w:
        cp.wait()

    def w_fwd(j, h, tx):
        return rcopy(wbuf.at[j, h], wbuf.at[j, h], tx, w_rx.at[j, h], c_peer)

    for j in range(nr):
        @pl.when(j != r)
        def _():
            w_fwd(j, k, w_tx.at[j]).wait_recv()
            w_fwd(j, k, w_cs.at[j]).start()
    for j in range(nr):
        @pl.when(j != r)
        def _():
            w_fwd(j, 1 - k, w_tx.at[j]).wait_recv()

    tile = 256
    for t in range(wbuf.shape[3] // tile):
        cols = slice(t * tile, (t + 1) * tile)
        w_tile = wbuf[:, :, :, cols].reshape(heads * HD, tile)
        proj_ref[:, :, cols] = (
            jnp.dot(att[...], w_tile, preferred_element_type=F32)
            .astype(BF16).reshape(2, rows, tile)
        )

    for j in range(nr):
        c_fwd(c_slot(j, 1 - y, k), c_rs.at[0], c_peer).wait_recv()
        c_fwd(c_slot(j, 1 - y, k), c_cs.at[2 * j + 1], c_peer).start()
    for j in range(nr):
        for yy in range(2):
            c_fwd(c_slot(j, yy, 1 - k), c_rs.at[0], c_peer).wait_recv()
    for j in range(nr):
        for q in range(4):
            i = j * 4 + q

            @pl.when(i != me)
            def _():
                rcopy(abuf.at[i], abuf.at[i], a_tx.at[i], a_rx.at[i], c_peer).wait_recv()

    def g_copy(zz):
        return rcopy(
            gbuf.at[zz], rbuf.at[z], g_tx.at[zz], g_rx.at[z], seq_id(zz, y, k)
        )

    lhs = jnp.concatenate([abuf[i] for i in range(grp)], axis=1)
    for cb in range(nc):
        rhs = cbuf[:, :, :, cb * cc:(cb + 1) * cc].reshape(grp * qn, cc)
        g_tile = jnp.dot(lhs, rhs, preferred_element_type=F32).astype(BF16)
        for rr in range(nz // nc):
            zz = rr * nc + cb
            gbuf[zz] = g_tile[rr * cr:(rr + 1) * cr]

            @pl.when(zz != z)
            def _():
                g_copy(zz).start()

            @pl.when(zz == z)
            def _():
                rbuf[zz] = g_tile[rr * cr:(rr + 1) * cr]

    total = jnp.zeros((cr, cc), F32)
    for zz in range(nz):
        @pl.when(zz != z)
        def _():
            rcopy(rbuf.at[zz], rbuf.at[zz], g_tx.at[zz], g_rx.at[zz], c_peer).wait_recv()

        total = total + rbuf[zz].astype(F32)

    def region(zz, yy, kk):
        return fbuf.at[seq_id(zz, yy, kk)]

    fbuf[s] = total.astype(BF16)

    def f_copy(zz, yy, kk, tx, peer):
        return rcopy(
            region(zz, yy, kk), region(zz, yy, kk), tx, f_rx.at[seq_id(zz, yy, kk)], peer
        )

    def f_z(zz):
        return f_copy(z, y, k, f_zs.at[zz], seq_id(zz, y, k))

    for zz in range(nz):
        @pl.when(zz != z)
        def _():
            f_z(zz).start()
    f_copy(z, y, k, f_ys.at[z], y_peer).start()
    f_copy(z, y, k, f_cs.at[2 * z + y], c_peer).start()
    for zz in range(nz):
        @pl.when(zz != z)
        def _():
            f_copy(zz, y, k, f_ys.at[zz], y_peer).wait_recv()
            f_copy(zz, y, k, f_ys.at[zz], y_peer).start()
            f_copy(zz, y, k, f_cs.at[2 * zz + y], c_peer).start()
    for zz in range(nz):
        f_copy(zz, 1 - y, k, f_cs.at[0], c_peer).wait_recv()
        f_copy(zz, 1 - y, k, f_cs.at[2 * zz + 1 - y], c_peer).start()
    for zz in range(nz):
        for yy in range(2):
            f_copy(zz, yy, 1 - k, f_cs.at[0], c_peer).wait_recv()

    for slot in range(ns):
        zz, q = slot // 4, slot % 4
        row = q * slice_rows + (zz // nc) * cr
        col = (zz % nc) * cc
        wg_ref[row:row + cr, col:col + cc] = fbuf[slot]

    @pl.loop(z + 1, nz)
    def _(zz):
        kv_z(zz).wait_send()

    @pl.when(z > 0)
    def _():
        kv_z(z - 1).wait_send()

    for zz in range(nz):
        @pl.when(zz <= z + 1)
        def _():
            kv_y(zz).wait_send()
            kv_c(zz, 0).wait_send()
            kv_c(zz, 1).wait_send()

    for step, i in noisy_steps:
        @pl.when(inside(step))
        def _():
            noisy_tx(step, i).wait_send()
    noisy_c(own_noisy, 1, 2).wait_send()
    noisy_relay(True)
    for j in range(nr):
        @pl.when(j != r)
        def _():
            c_rep(j).wait_send()
            w_rep(j).wait_send()
            w_fwd(j, k, w_cs.at[j]).wait_send()
        c_fwd(c_slot(j, y, k), c_ys.at[j], y_peer).wait_send()
        for h in range(2):
            c_fwd(c_slot(j, h, k), c_cs.at[2 * j + h], c_peer).wait_send()
        for q in range(4):
            @pl.when(j * 4 + q != me)
            def _():
                a_copy(j, q).wait_send()
    for zz in range(nz):
        @pl.when(zz != z)
        def _():
            g_copy(zz).wait_send()
            f_z(zz).wait_send()
        f_copy(zz, y, k, f_ys.at[zz], y_peer).wait_send()
        for yy in range(2):
            f_copy(zz, yy, k, f_cs.at[2 * zz + yy], c_peer).wait_send()


def on_device(queries, keys_values, block_lengths, out_weight, cotangent):
    ns, nr = lax.axis_size("seq"), lax.axis_size("rep")
    nz = ns // 4
    rows, q_width = queries.shape[2], queries.shape[3]
    kv_width = keys_values.shape[4]
    w_rows, out_width = out_weight.shape
    kvh, gs = kv_width // HD, q_width // kv_width
    qn = 2 * rows
    lanes = gs * qn
    slice_rows = w_rows // 4
    nc = min(nz, out_width // 128)
    cr, cc = slice_rows // (nz // nc), out_width // nc
    dma = pltpu.SemaphoreType.DMA
    vmem, hbm = pl.BlockSpec(memory_space=pltpu.VMEM), pl.BlockSpec(memory_space=pl.ANY)
    projected, grad = pl.pallas_call(
        functools.partial(kernel, ns, nr, nc),
        out_shape=(
            jax.ShapeDtypeStruct((2, rows, out_width), BF16),
            jax.ShapeDtypeStruct((w_rows, out_width), BF16),
        ),
        in_specs=[pl.BlockSpec(memory_space=pltpu.SMEM), vmem, hbm, hbm, hbm],
        out_specs=(vmem, vmem),
        scratch_shapes=[
            pltpu.VMEM((ns, 2, rows, kv_width), BF16),
            pltpu.VMEM((5, 2, rows, kv_width), BF16),
            pltpu.VMEM((nr, 2, w_rows // 2, out_width), BF16),
            pltpu.VMEM((4 * nr, 2, rows, out_width), BF16),
            pltpu.VMEM((4 * nr, slice_rows, qn), BF16),
            pltpu.VMEM((q_width, qn), BF16),
            pltpu.VMEM((qn, q_width), BF16),
            pltpu.VMEM((kvh, HD, lanes), F32),
            pltpu.VMEM((kvh, 1, lanes), F32),
            pltpu.VMEM((kvh, 1, lanes), F32),
            pltpu.VMEM((nz, cr, cc), BF16),
            pltpu.VMEM((nz, cr, cc), BF16),
            pltpu.VMEM((ns, cr, cc), BF16),
            dma((5,)),
            dma((ns,)), dma((nz,)), dma((nz,)), dma((ns // 2,)),
            dma((5,)), dma((4,)),
            dma((nr, 2)), dma((nr,)), dma((nr,)),
            dma((4 * nr,)), dma((nr,)), dma((nr,)), dma((2 * nr,)),
            dma((4 * nr,)), dma((4 * nr,)),
            dma((nz,)), dma((nz,)),
            dma((ns,)), dma((nz,)), dma((nz,)), dma((ns // 2,)),
        ],
        compiler_params=pltpu.CompilerParams(
            collective_id=0, has_side_effects=True, vmem_limit_bytes=60 * 2**20
        ),
    )(block_lengths, queries[0], keys_values, out_weight, cotangent)
    return projected[None], grad.astype(F32)


def solution(mesh):
    placed = (
        P("rep", None, "seq", None),
        P("rep", None, None, "seq", None),
        P("rep", None),
        P("rep", None),
        P("rep", None, "seq", None),
    )
    return jax.shard_map(
        on_device,
        mesh=mesh,
        in_specs=placed,
        out_specs=(P("rep", None, "seq", None), P("rep", None)),
        check_vma=False,
    )
```
